256 devices in a mesh: kv: 8 (over y, z_hi), ex: 32 (over z_lo, x, core).
Axes of the slice: x: 4, y: 4, z: 8 (z_hi: 2, z_lo: 4; z = z_hi * 4 + z_lo), core: 2. Of those that a mesh axis runs over, the one named last changes fastest.
Arguments:
- x_tokens: bfloat16 [32, 576, 2048], P('ex'), may hold values from -6 to 6
- attn_gain: float32 [2048], replicated, may hold values from 0.1 to 1.9
- w_qkv: bfloat16 [2048, 3, 2048], P(None, None, 'kv'), may hold values from -1 to 1
- w_out: bfloat16 [2048, 2048], P('kv'), may hold values from -0.125 to 0.125
- cache: bfloat16 [64, 2, 512, 2048], P('ex', None, None, 'kv'), may hold values from -6 to 6
- cache_len: int32 [64], P('ex'), may hold values from 1 to 512, 16384 in all
- moe_gain: float32 [2048], replicated, may hold values from 0.1 to 1.9
- w_trainer: float32 [32, 3, 2048, 1024], P(None, None, 'ex', 'kv'), may hold values from -0.125 to 0.125
- expert_ids: int32 [32, 576, 8], P('ex', 'kv'), may hold values from 0 to 31, all different within a row; in each aligned block of 72 rows (0 to 71, 72 to 143, ..., all dimensions but the last counted through in order) at most 28 rows name the same one
- route_probs: float32 [32, 576, 8], P('ex', 'kv'), may hold values from 0.05 to 1
Outputs:
- layer_out: bfloat16 [32, 576, 2048], P('ex', 'kv')
The draws below stay inside these ranges and needn't reach their ends.
Inputs may be any that keep to these rules, and one draw needn't show every extreme that they name: `expert_ids`: in each aligned block of 72 tokens, no expert is named by more than 28 of them; each token names 8 different experts.
All inputs are finite; a program needn't handle non-finite values. No bound on the sum of `cache_len` on one device may be relied on, other than what follows from the above.
Results may differ from the reference program's by a relative error of at most 0.0055.
Values may be sent and summed in bfloat16 or wider, within the bound.
A program may use at most 128 MiB of HBM per device.

```python
import math
import jax
import jax.numpy as jnp
import numpy as np
from jax import lax

D = 2048
H = 16
HD = 128
FF = 1024
TOPK = 8
PLEN = 512
REQ_DEV = 2
QB = 32
CMAX = 512
EXPERTS = 32
GROUPS = 32
REQUESTS = 64
ROWS = 576
ROWS_DEV = 72
CAP = 28


def draw_w_qkv(key, part):
    base = jax.random.normal(key, (D, 3, H * HD), jnp.float32) / math.sqrt(D)
    return jnp.clip(base, -1.0, 1.0).astype(jnp.bfloat16)


def levels(key, shape, shards, least, top_value):
    def one(dim, shards_of):
        draws = jax.random.uniform(jax.random.fold_in(jax.random.fold_in(key, 6), dim), (shards_of,), jnp.float32, least / len(shards), top_value / len(shards))
        return jnp.repeat(jnp.exp(draws), shape[dim] // shards_of).reshape((-1,) + (1,) * (len(shape) - dim - 1))

    level = one(*shards[0])
    for cut in shards[1:]:
        level = level * one(*cut)
    return level


def profile(number_of, total, bound, slope):
    loads = [(1 << 20) // math.isqrt(standing ** slope) + 1 for standing in range(2, number_of + 1)]
    spare, given = total - bound - (number_of - 1), [1] * (number_of - 1)
    while spare > 0:
        free = [i for i in range(number_of - 1) if given[i] < bound]
        pool, remaining = sum([loads[i] for i in free]), spare
        for i in free:
            addition = min(bound - given[i], max(1, remaining * loads[i] // pool), spare)
            given[i] = given[i] + addition
            spare = spare - addition
    return np.array([bound] + given)


def ragged(own_key, count, total, reach, lean):
    if count == 2:
        one = jax.random.randint(own_key, (), max(1, total - reach), min(reach, total - 1) + 1)
        return jnp.stack([one, total - one])
    sizes = jnp.asarray(profile(count, total, reach, lean), jnp.int32)
    couples = (count - 1) // 2
    giver, taker = sizes[1:1 + 2 * couples:2], sizes[2:2 + 2 * couples:2]
    room = jnp.minimum(giver - 1, reach - taker)
    shifted = jax.random.randint(jax.random.fold_in(own_key, 1), (couples,), 0, 1 << 20) % (room + 1)
    sizes = sizes.at[1:1 + 2 * couples:2].set(giver - shifted).at[2:2 + 2 * couples:2].set(taker + shifted)
    return sizes[jax.random.permutation(jax.random.fold_in(own_key, 2), count)]


def shared_out(own_key, own, number, rows, count, top, limit, lean):
    sequence = jax.random.permutation(own_key, count)
    packed, usual = portions_of(count, rows * top, limit, lean, True), portions_of(count, rows * top, limit, lean, False)
    places = jnp.arange(count)

    def named(tallies, turn):
        used = int((tallies > 0).sum())
        fixed = max(1, used // 4)
        passed = fixed + (places - fixed + turn * (used - fixed)) % max(1, count - fixed)
        return jnp.zeros((count,), jnp.int32).at[sequence[jnp.where(places < fixed, places, passed)]].set(jnp.asarray(tallies, jnp.int32))

    tallies = jnp.where(number % 4 == 0, named(packed, number // 4), named(usual, number - number // 4 - 1))
    mixed = jax.random.permutation(jax.random.fold_in(own, 3), count)
    source_of, sink = mixed[0:count // 2 * 2:2], mixed[1:count // 2 * 2:2]
    slack = jnp.minimum(tallies[source_of] - 1, limit - tallies[sink]) // 2
    slack = jnp.where((source_of == sequence[0]) | (sink == sequence[0]) | (tallies[sink] == 0), 0, jnp.maximum(slack, 0))
    passed = jax.random.randint(jax.random.fold_in(own, 4), (count // 2,), 0, 1 << 20) % (slack + 1)
    tallies = tallies.at[source_of].add(-passed).at[sink].add(passed)
    members = jnp.searchsorted(jnp.cumsum(tallies), jnp.arange(rows * top), side="right").astype(jnp.int32)
    table = members.reshape(top, rows).T
    table = table[jax.random.permutation(jax.random.fold_in(own, 1), rows)]
    turn = jax.random.randint(jax.random.fold_in(own, 2), (rows, 1), 0, top)
    return jnp.take_along_axis(table, (jnp.arange(top)[None, :] + turn) % top, axis=1)


def portions_of(amount, total, bound, lean, full):
    loads = [(1 << 20) // math.isqrt(grade ** lean) + 1 for grade in range(1, amount + 1)]
    largest = bound if full else min(bound, max(-(-total // amount), total * loads[0] // sum(loads)))
    least = 1 if total - largest >= amount - 1 else 0
    given, surplus = [largest] + [least] * (amount - 1), total - largest - least * (amount - 1)
    while surplus > 0:
        candidates = [i for i in range(1, amount) if given[i] < largest] or [i for i in range(1, amount) if given[i] < bound]
        pool, budget = sum([loads[i] for i in candidates]), surplus
        for i in candidates:
            more = min(bound - given[i], max(1, budget * loads[i] // pool), surplus)
            given[i] = given[i] + more
            surplus = surplus - more
    return np.array(given)


def noise(stream_key, extent, deviation, reach, split=(), kind=jnp.bfloat16):
    entries = jax.random.normal(stream_key, extent, jnp.float32) * deviation
    if len(split) > 0:
        entries = levels(stream_key, extent, split, -0.22, 0.18) * entries
    return jnp.clip(entries, min=-reach, max=reach).astype(kind)


def setup_inputs(seed: int = 0) -> dict:
    arg_keys = jax.random.split(jax.random.key(seed), 11)
    x_tokens = noise(arg_keys[0], (GROUPS, ROWS, D), 1.0, 6.0, ((0, 32),))
    attn_gain = jnp.clip(1.0 + 0.18 * jax.random.normal(arg_keys[1], (D,), jnp.float32), 0.1, 1.9)
    w_qkv = draw_w_qkv(jax.random.fold_in(arg_keys[10], 71), 0)
    w_out = noise(arg_keys[3], (H * HD, D), (H * HD) ** -0.5, 0.125, ((0, 8),))
    cache = noise(arg_keys[4], (REQUESTS, 2, CMAX, H * HD), 1.0, 6.0, ((0, 32), (3, 8)))
    cache_len = ragged(arg_keys[5], REQUESTS, REQUESTS * CMAX // 2, CMAX, 2).astype(jnp.int32)
    moe_gain = jnp.clip(1.0 + 0.18 * jax.random.normal(arg_keys[6], (D,), jnp.float32), 0.1, 1.9)
    w_trainer = noise(arg_keys[7], (EXPERTS, 3, D, FF), D ** -0.5, 0.125, ((2, 32), (3, 8)), jnp.float32)
    expert_ids_keys = jax.random.split(jax.random.fold_in(arg_keys[8], 1), GROUPS * ROWS // ROWS_DEV)
    expert_ids_turns = jax.random.permutation(jax.random.fold_in(arg_keys[8], 3), GROUPS * ROWS // ROWS_DEV)
    expert_ids = jax.vmap(lambda own, number: shared_out(jax.random.fold_in(arg_keys[8], 2), own, number, ROWS_DEV, EXPERTS, TOPK, CAP, 2))(expert_ids_keys, expert_ids_turns).reshape((GROUPS, ROWS, TOPK))
    route_probs = jnp.clip(jnp.exp(math.log(1.0) - 2.9957323 * jax.random.uniform(arg_keys[9], (GROUPS, ROWS, TOPK), jnp.float32) ** levels(arg_keys[9], (GROUPS, ROWS, TOPK), ((0, 32), (1, 8)), -0.2, 0.2)), 0.05, 1.0)
    return dict(x_tokens=x_tokens, attn_gain=attn_gain, w_qkv=w_qkv, w_out=w_out, cache=cache, cache_len=cache_len, moe_gain=moe_gain, w_trainer=w_trainer, expert_ids=expert_ids, route_probs=route_probs)


block_rows = 512

def rms_scale(rows, gain):
    values = rows.astype(jnp.float32)
    scale = lax.rsqrt(lax.optimization_barrier(jnp.mean(values * values, axis=-1, keepdims=True)) + 1e-06)
    return values * scale * gain.astype(jnp.float32)

def attend(query, keys, values, valid):
    scores = jnp.einsum('qhd,khd->hqk', query.astype(jnp.float32), keys.astype(jnp.float32)) / math.sqrt(HD)
    scores = jnp.where(valid[None, None, :], scores, -1e+30)
    top = lax.optimization_barrier(jnp.max(scores, axis=-1, keepdims=True))
    weights = jnp.exp(scores - top)
    probs = (weights / lax.optimization_barrier(jnp.sum(weights, axis=-1, keepdims=True))).astype(jnp.bfloat16)
    mixed = jnp.einsum('hqk,khd->qhd', probs.astype(jnp.float32), values.astype(jnp.float32))
    return mixed.astype(jnp.bfloat16)

def reference(x_tokens, attn_gain, w_qkv, w_out, cache, cache_len, moe_gain, w_trainer, expert_ids, route_probs):
    server = w_trainer.astype(jnp.bfloat16)
    flat_qkv = w_qkv.reshape(D, 3 * H * HD)
    lengths_all = cache_len.reshape(GROUPS, REQ_DEV)
    stores = cache.reshape(GROUPS, REQ_DEV, 2, CMAX, H * HD)

    def group(items):
        rows, lengths, store = items
        normed = rms_scale(rows, attn_gain).astype(jnp.bfloat16)
        proj = jnp.dot(normed, flat_qkv, preferred_element_type=jnp.float32).astype(jnp.bfloat16)
        proj = proj.reshape(ROWS, 3, H, HD)
        query, keys, values = (proj[:, 0], proj[:, 1], proj[:, 2])
        prompt_out = attend(query[:PLEN], keys[:PLEN], values[:PLEN], jnp.ones((PLEN,), dtype=bool))
        req_q = query[PLEN:].reshape(REQ_DEV, QB, H, HD)
        req_k = keys[PLEN:].reshape(REQ_DEV, QB, H, HD)
        req_v = values[PLEN:].reshape(REQ_DEV, QB, H, HD)
        all_k = jnp.concatenate([req_k, store[:, 0].reshape(REQ_DEV, CMAX, H, HD)], axis=1)
        all_v = jnp.concatenate([req_v, store[:, 1].reshape(REQ_DEV, CMAX, H, HD)], axis=1)
        live = jnp.arange(CMAX, dtype=jnp.int32)[None, :] < lengths[:, None]
        valid = jnp.concatenate([jnp.ones((REQ_DEV, QB), dtype=bool), live], axis=1)
        req_out = jax.vmap(attend)(req_q, all_k, all_v, valid)
        heads_out = jnp.concatenate([prompt_out, req_out.reshape(REQ_DEV * QB, H, HD)], axis=0)
        heads_out = heads_out.reshape(ROWS, H * HD)
        attn = jnp.dot(heads_out, w_out, preferred_element_type=jnp.float32)
        return rows.astype(jnp.float32) + attn
    resid = lax.map(group, (x_tokens, lengths_all, stores))
    flat_res = resid.reshape(GROUPS * ROWS, D)
    moe_in = rms_scale(flat_res, moe_gain).astype(jnp.bfloat16)
    probs = route_probs.reshape(-1, TOPK)
    share = (probs / lax.optimization_barrier(jnp.sum(probs, axis=-1, keepdims=True))).reshape(-1)
    keys_flat = expert_ids.reshape(-1).astype(jnp.int32)
    order = jnp.argsort(keys_flat, stable=True).astype(jnp.int32)
    counts = lax.optimization_barrier(jnp.sum((keys_flat[:, None] == jnp.arange(EXPERTS, dtype=jnp.int32)[None, :]).astype(jnp.int32), axis=0))
    starts = (jnp.cumsum(counts) - counts).astype(jnp.int32)
    order_pad = jnp.concatenate([order, jnp.zeros((block_rows,), jnp.int32)])

    def expert_step(expert, total):
        weights = server[expert]

        def block_step(index, total):
            begin = (starts[expert] + index * block_rows).astype(jnp.int32)
            picks = lax.dynamic_slice(order_pad, (begin,), (block_rows,))
            live = index * block_rows + jnp.arange(block_rows, dtype=jnp.int32) < counts[expert]
            tokens = picks // TOPK
            rows = moe_in[tokens]
            gate = jnp.dot(rows, weights[0], preferred_element_type=jnp.float32)
            up = jnp.dot(rows, weights[1], preferred_element_type=jnp.float32)
            hidden = (jax.nn.silu(gate) * up).astype(jnp.bfloat16)
            result = lax.dot_general(hidden, weights[2], (((1,), (1,)), ((), ())), preferred_element_type=jnp.float32)
            result = result.astype(jnp.bfloat16)
            factor = jnp.where(live, share[picks], jnp.zeros((block_rows,), jnp.float32))
            return total.at[tokens].add(factor[:, None] * result.astype(jnp.float32))
        blocks = (counts[expert] + block_rows - 1) // block_rows
        return lax.fori_loop(0, blocks, block_step, total)
    total = lax.fori_loop(0, EXPERTS, expert_step, jnp.zeros((GROUPS * ROWS, D), jnp.float32))
    return (flat_res + total).astype(jnp.bfloat16).reshape(GROUPS, ROWS, D)
```

```python
import math

import jax
import jax.numpy as jnp
from jax import lax
from jax.experimental import pallas as pl
from jax.experimental.pallas import tpu as pltpu
from jax.sharding import PartitionSpec as P

HD = 128
TOPK = 8
PLEN = 512
REQ_DEV = 2
QB = 32
CMAX = 512


MESH = pl.DeviceIdType.MESH


def position():
    kv, ex = lax.axis_index("kv"), lax.axis_index("ex")
    return (ex // 2) % 4, kv // 2, (kv % 2) * 4 + ex // 8, ex % 2


def device(x, y, z, c):
    x, y, z, c = (x + 8) % 4, (y + 8) % 4, (z + 16) % 8, c % 2
    return y * 2 + z // 4, ((z % 4) * 4 + x) * 2 + c


def same_y(k):
    return [(dx, k, dc) for dx in (1, 3, 2, 0) for dc in (0, 1)]


def weights_kernel(own_ref, out_ref, send_sem, recv_sem, ysend_sem, yrecv_sem):
    x, y, z, c = position()
    kv, ex = device(x, y, z, c)
    rows = own_ref.shape[2]
    barrier = pltpu.get_barrier_semaphore()

    @pl.loop(0, 8)
    def _(k):
        for dx in range(4):
            for dc in range(2):
                if dx or dc:
                    pl.semaphore_signal(
                        barrier, inc=1, device_id=device(x + dx, y, z + k, c + dc), device_id_type=MESH
                    )

    @pl.loop(1, 8)
    def _(k):
        pl.semaphore_signal(barrier, inc=1, device_id=device(x, y, z + k, c), device_id_type=MESH)

    for dy in (1, 2, 3):
        pl.semaphore_signal(barrier, inc=1, device_id=device(x, y + dy, z, c), device_id_type=MESH)
    pl.semaphore_wait(barrier, 66)

    def piece(k, dx, dc):
        dz = (3 * k) % 8
        to = device(x + dx, y, z + dz, c + dc)
        return pltpu.make_async_remote_copy(
            src_ref=own_ref.at[to[1]],
            dst_ref=out_ref.at[kv, :, pl.ds(pl.multiple_of(ex * rows, rows), rows), :],
            send_sem=send_sem.at[k],
            recv_sem=recv_sem.at[k],
            device_id=to,
            device_id_type=MESH,
        )

    local = pltpu.make_async_copy(
        own_ref.at[ex],
        out_ref.at[kv, :, pl.ds(pl.multiple_of(ex * rows, rows), rows), :],
        recv_sem.at[0],
    )
    local.start()
    for dx in (1, 3, 2, 0):
        for dc in (0, 1):
            if dx or dc:
                piece(0, dx, dc).start()

    @pl.loop(1, 8)
    def _(k):
        for dx in (1, 3, 2, 0):
            for dc in (0, 1):
                piece(k, dx, dc).start()

    whole = 8 * rows

    def group(k):
        dz = (3 * k) % 8
        zs = (z + 8 - dz) % 8
        first = pl.multiple_of((zs % 4) * whole, whole)
        return out_ref.at[y * 2 + zs // 4, :, pl.ds(first, whole), :]

    def spread(k, dy):
        return pltpu.make_async_remote_copy(
            src_ref=group(k),
            dst_ref=group(k),
            send_sem=ysend_sem.at[dy, k],
            recv_sem=yrecv_sem.at[dy, k],
            device_id=device(x, y + dy, z, c),
            device_id_type=MESH,
        )

    @pl.loop(0, 8)
    def _(k):
        pltpu.make_async_copy(group(k), group(k), recv_sem.at[k]).wait()
        for dy in (1, 3, 2):
            spread(k, dy).start()

    def sent(k, count):
        part = own_ref.at[pl.ds(0, count)]
        pltpu.make_async_copy(part, part, send_sem.at[k]).wait()

    sent(0, 7)

    @pl.loop(1, 8)
    def _(k):
        sent(k, 8)

    @pl.loop(0, 8)
    def _(k):
        for dy in (1, 2, 3):
            spread(k, dy).wait()


def gather_weights(own):
    experts, three, rows, cols = own.shape
    return pl.pallas_call(
        weights_kernel,
        out_shape=jax.ShapeDtypeStruct((8, three, 32 * rows, cols), own.dtype),
        in_specs=[pl.BlockSpec(memory_space=pltpu.VMEM)],
        out_specs=pl.BlockSpec(memory_space=pl.ANY),
        scratch_shapes=[
            pltpu.SemaphoreType.DMA((8,)),
            pltpu.SemaphoreType.DMA((8,)),
            pltpu.SemaphoreType.DMA((4, 8)),
            pltpu.SemaphoreType.DMA((4, 8)),
        ],
        compiler_params=pltpu.CompilerParams(collective_id=0, has_side_effects=True),
        name="gather_weights",
    )(own)


def rms_scale(rows, gain):
    values = rows.astype(jnp.float32)
    scale = lax.rsqrt(jnp.mean(values * values, axis=-1, keepdims=True) + 1e-06)
    return values * scale * gain


def attend(query, keys, values, valid):
    scores = jnp.einsum(
        "qhd,khd->hqk", query, keys, preferred_element_type=jnp.float32
    ) / math.sqrt(HD)
    scores = jnp.where(valid[None, None, :], scores, -1e30)
    top = jnp.max(scores, axis=-1, keepdims=True)
    weights = jnp.exp(scores - top)
    probs = (weights / jnp.sum(weights, axis=-1, keepdims=True)).astype(jnp.bfloat16)
    mixed = jnp.einsum("hqk,khd->qhd", probs, values, preferred_element_type=jnp.float32)
    return mixed.astype(jnp.bfloat16)


def on_device(
    x_tokens,
    attn_gain,
    w_qkv,
    w_out,
    cache,
    cache_len,
    moe_gain,
    w_trainer,
    expert_ids,
    route_probs,
):
    trainer = w_trainer.astype(jnp.bfloat16)
    whole = gather_weights(trainer)
    server = whole.transpose(1, 2, 0, 3).reshape(1, 3, x_tokens.shape[2], -1)
    rows = x_tokens[0]
    row_count = rows.shape[0]
    local_heads = w_qkv.shape[2] // HD
    normed = rms_scale(rows, attn_gain).astype(jnp.bfloat16)
    flat_qkv = w_qkv.reshape(w_qkv.shape[0], 3 * local_heads * HD)
    proj = jnp.dot(normed, flat_qkv, preferred_element_type=jnp.float32).astype(jnp.bfloat16)
    proj = proj.reshape(row_count, 3, local_heads, HD)
    query, keys, values = (proj[:, 0], proj[:, 1], proj[:, 2])
    prompt_out = attend(query[:PLEN], keys[:PLEN], values[:PLEN], jnp.ones((PLEN,), dtype=bool))
    req_q = query[PLEN:].reshape(REQ_DEV, QB, local_heads, HD)
    req_k = keys[PLEN:].reshape(REQ_DEV, QB, local_heads, HD)
    req_v = values[PLEN:].reshape(REQ_DEV, QB, local_heads, HD)
    all_k = jnp.concatenate([req_k, cache[:, 0].reshape(REQ_DEV, CMAX, local_heads, HD)], axis=1)
    all_v = jnp.concatenate([req_v, cache[:, 1].reshape(REQ_DEV, CMAX, local_heads, HD)], axis=1)
    live = jnp.arange(CMAX, dtype=jnp.int32)[None, :] < cache_len[:, None]
    valid = jnp.concatenate([jnp.ones((REQ_DEV, QB), dtype=bool), live], axis=1)
    req_out = jax.vmap(attend)(req_q, all_k, all_v, valid)
    heads_out = jnp.concatenate(
        [prompt_out, req_out.reshape(REQ_DEV * QB, local_heads, HD)], axis=0
    )
    heads_out = heads_out.reshape(row_count, local_heads * HD)
    rows_dev = row_count // lax.axis_size("kv")
    mixed = lax.psum_scatter(
        jnp.dot(heads_out, w_out, preferred_element_type=jnp.float32),
        "kv",
        scatter_dimension=0,
        tiled=True,
    )
    own_rows = lax.dynamic_slice_in_dim(rows, lax.axis_index("kv") * rows_dev, rows_dev, 0)
    resid = own_rows.astype(jnp.float32) + mixed
    moe_in = rms_scale(resid, moe_gain).astype(jnp.bfloat16)
    experts = w_trainer.shape[0]
    width = moe_in.shape[1]
    chosen = expert_ids[0]
    probs = route_probs[0]
    share = probs / jnp.sum(probs, axis=-1, keepdims=True)
    slot_cap = max(2, 8 * rows_dev * TOPK // (5 * experts))
    flat_ids = chosen.reshape(-1)
    onehot = (flat_ids[:, None] == jnp.arange(experts, dtype=jnp.int32)[None, :]).astype(jnp.int32)
    before = jnp.cumsum(onehot, axis=0) - onehot
    place = jnp.sum(before * onehot, axis=1)
    slot = flat_ids * slot_cap + place
    match = jnp.arange(experts * slot_cap, dtype=jnp.int32)[:, None] == slot[None, :]
    spread = jnp.sum(match.reshape(experts * slot_cap, rows_dev, TOPK).astype(jnp.float32), axis=-1)
    send = jnp.dot(spread.astype(jnp.bfloat16), moe_in, preferred_element_type=jnp.float32)
    send = send.astype(jnp.bfloat16).reshape(experts, slot_cap, width)
    block = lax.all_to_all(send, "ex", split_axis=0, concat_axis=0, tiled=True)
    sources = block.shape[0]
    slots = block.shape[1]
    flat_rows = block.reshape(sources * slots, width)
    gate = jnp.dot(flat_rows, server[0, 0], preferred_element_type=jnp.float32)
    up = jnp.dot(flat_rows, server[0, 1], preferred_element_type=jnp.float32)
    hidden = (jax.nn.silu(gate) * up).astype(jnp.bfloat16)
    result = lax.dot_general(
        hidden, server[0, 2], (((1,), (1,)), ((), ())), preferred_element_type=jnp.float32
    )
    result = result.astype(jnp.bfloat16).reshape(sources, slots, width)
    returned = lax.all_to_all(result, "ex", split_axis=0, concat_axis=0, tiled=True)
    table = returned.reshape(experts * slot_cap, width)
    picked = jnp.take(table, slot.reshape(rows_dev, TOPK), axis=0)
    moe_out = jnp.sum(share[:, :, None] * picked.astype(jnp.float32), axis=1)
    return (resid + moe_out).astype(jnp.bfloat16)[None]


def solution(mesh):
    return jax.shard_map(
        on_device,
        mesh=mesh,
        in_specs=(
            P("ex", None, None),
            P(),
            P(None, None, "kv"),
            P("kv", None),
            P("ex", None, None, "kv"),
            P("ex"),
            P(),
            P(None, None, "ex", "kv"),
            P("ex", "kv", None),
            P("ex", "kv", None),
        ),
        out_specs=P("ex", "kv", None),
        check_vma=False,
    )
```

```python
import math

import jax
import jax.numpy as jnp
from jax import lax
from jax.experimental import pallas as pl
from jax.experimental.pallas import tpu as pltpu
from jax.sharding import PartitionSpec as P

HD = 128
TOPK = 8
PLEN = 512
REQ_DEV = 2
QB = 32
CMAX = 512
EXPERTS = 32
CAP = 28
WIDTH = 2048
ROWS = 576
OWN = 72
PAIR = 2 * CAP
SLOTS = 8 * PAIR
WIDE = 512
MESH = pl.DeviceIdType.MESH
F32 = jnp.float32
BF16 = jnp.bfloat16


def position():
    kv, ex = lax.axis_index("kv"), lax.axis_index("ex")
    return (ex // 2) % 4, kv // 2, (kv % 2) * 4 + ex // 8, ex % 2


def device(x, y, z, c):
    x, y, z, c = (x + 8) % 4, (y + 8) % 4, (z + 16) % 8, c % 2
    return y * 2 + z // 4, ((z % 4) * 4 + x) * 2 + c


def send_to(src, dst, send_sem, recv_sem, to):
    return pltpu.make_async_remote_copy(
        src_ref=src, dst_ref=dst, send_sem=send_sem, recv_sem=recv_sem, device_id=to, device_id_type=MESH
    )


def wait_bytes(ref, sem):
    pltpu.make_async_copy(ref, ref, sem).wait()


def times(a, b, contract=((1,), (0,))):
    return lax.dot_general(a, b, (contract, ((), ())), preferred_element_type=F32)


def softmax(parts):
    top = parts[0].max(axis=-1, keepdims=True)
    for part in parts[1:]:
        top = jnp.maximum(top, part.max(axis=-1, keepdims=True))
    parts = [jnp.exp(part - top) for part in parts]
    total = parts[0].sum(axis=-1, keepdims=True)
    for part in parts[1:]:
        total = total + part.sum(axis=-1, keepdims=True)
    return [(part / total).astype(BF16) for part in parts]


def layer_kernel(
    own_w, x_ref, own_x, attn_gain, w_qkv, w_out, cache, bias, moe_gain, route,
    out_ref,
    wbuf, proj, heads, part, y_out, y_in, z_out, z_in, resid, ztok, zroute, packs, slots, total, rback, c_out, c_in,
    a_send, a_recv, s_send, s_recv, r_send, r_recv, y_send, y_recv, z_send, z_recv,
    t_send, t_recv, m_send, m_recv, p_send, p_recv, b_send, b_recv, c_send, c_recv,
):
    x, y, z, c = position()
    kv, ex = device(x, y, z, c)
    zl, zh = z % 4, z // 4
    piece_rows = own_w.shape[2]
    barrier = pltpu.get_barrier_semaphore()

    @pl.loop(0, 8)
    def _(k):
        for dx in range(4):
            for dc in range(2):
                if dx or dc:
                    pl.semaphore_signal(
                        barrier, inc=1, device_id=device(x + dx, y, z + k, c + dc), device_id_type=MESH
                    )

    @pl.loop(1, 8)
    def _(k):
        pl.semaphore_signal(barrier, inc=1, device_id=device(x, y, z + k, c), device_id_type=MESH)

    for dy in (1, 2, 3):
        pl.semaphore_signal(barrier, inc=1, device_id=device(x, y + dy, z, c), device_id_type=MESH)
    pl.semaphore_wait(barrier, 66)

    def route_copy(r):
        return send_to(
            route.at[(zl + r) % 4], zroute.at[zl], m_send.at[r], m_recv.at[r],
            device(x, y, zh * 4 + (zl + r) % 4, c),
        )

    for r in (1, 2, 3):
        route_copy(r).start()
    own_route = pltpu.make_async_copy(route.at[zl], zroute.at[zl], m_recv.at[0])
    own_route.start()

    own_rows = pl.ds(pl.multiple_of(ex * piece_rows, piece_rows), piece_rows)

    def piece(k, dx, dc):
        to = device(x + dx, y, z + (3 * k) % 8, c + dc)
        return send_to(own_w.at[to[1]], wbuf.at[kv, :, own_rows, :], a_send.at[k], a_recv.at[k], to)

    pltpu.make_async_copy(own_w.at[ex], wbuf.at[kv, :, own_rows, :], a_recv.at[0]).start()
    for dx in (1, 3, 2, 0):
        for dc in (0, 1):
            if dx or dc:
                piece(0, dx, dc).start()

    @pl.loop(1, 8)
    def _(k):
        for dx in (1, 3, 2, 0):
            for dc in (0, 1):
                piece(k, dx, dc).start()

    whole = 8 * piece_rows

    def group(k, dy, first=0, count=whole):
        zs = (z + 8 - (3 * k) % 8) % 8
        begin = pl.multiple_of((zs % 4) * whole + first, piece_rows)
        return wbuf.at[((y + dy) % 4) * 2 + zs // 4, :, pl.ds(begin, count), :]

    half = whole // 2

    def spread(k):
        wait_bytes(group(k, 0), a_recv.at[k])
        for way, dy in ((0, 1), (1, 3)):
            send_to(
                group(k, 0), group(k, 0), s_send.at[way, k], s_recv.at[way, k], device(x, y + dy, z, c)
            ).start()

    def relay(k):
        for way, dy in ((0, 1), (1, 3)):
            wait_bytes(group(k, 4 - dy), s_recv.at[way, k])
            passed = group(k, 4 - dy, way * half, half)
            send_to(passed, passed, r_send.at[way, k], r_recv.at[way, k], device(x, y + dy, z, c)).start()

    @pl.loop(0, 2)
    def _(i):
        rows = pl.ds(pl.multiple_of(i * (ROWS // 2), ROWS // 2), ROWS // 2)
        values = x_ref[rows, :].astype(F32)
        scale = lax.rsqrt(jnp.mean(values * values, axis=-1, keepdims=True) + 1e-06)
        normed = (values * scale * attn_gain[...]).astype(BF16)
        proj[rows, :] = times(normed, w_qkv[...]).astype(BF16)

    spread(0)

    def lanes(which, head):
        return pl.ds((which * 2 + head) * HD, HD)

    inv = 1.0 / math.sqrt(HD)
    tile = 128
    for head in range(2):
        @pl.loop(0, PLEN // tile)
        def _(i):
            rows = pl.ds(pl.multiple_of(i * tile, tile), tile)
            scores = times(proj[rows, lanes(0, head)], proj[0:PLEN, lanes(1, head)], ((1,), (1,))) * inv
            (probs,) = softmax([scores])
            heads[rows, pl.ds(head * HD, HD)] = times(probs, proj[0:PLEN, lanes(2, head)]).astype(BF16)

        for req in range(REQ_DEV):
            rows = pl.ds(PLEN + req * QB, QB)
            query = proj[rows, lanes(0, head)]
            near = times(query, proj[rows, lanes(1, head)], ((1,), (1,))) * inv
            far = times(query, cache[req, 0, :, pl.ds(head * HD, HD)], ((1,), (1,))) * inv
            far = far + bias[req:req + 1, :]
            near, far = softmax([near, far])
            mixed = times(near, proj[rows, lanes(2, head)]) + times(far, cache[req, 1, :, pl.ds(head * HD, HD)])
            heads[rows, pl.ds(head * HD, HD)] = mixed.astype(BF16)
        spread(1 + head)

    quarter = ROWS // 4

    def block(dy):
        return heads[pl.ds(pl.multiple_of(((y + dy) % 4) * quarter, quarter), quarter), :]

    def y_copy(dy):
        return send_to(y_out.at[dy], y_in.at[dy], y_send.at[dy], y_recv.at[dy], device(x, y + dy, z, c))

    for dy in (2, 1, 3):
        y_out[dy] = times(block(dy), w_out[...]).astype(BF16)
        y_copy(dy).start()
    part[...] = times(block(0), w_out[...])
    spread(3)
    relay(0)
    for dy in (1, 3, 2):
        y_copy(dy).wait_recv()
        part[...] += y_in[dy].astype(F32)
    z_out[...] = part[pl.ds(pl.multiple_of((1 - zh) * OWN, OWN), OWN), :].astype(BF16)
    z_copy = send_to(z_out, z_in, z_send, z_recv, device(x, y, z + 4, c))
    z_copy.start()
    spread(4)
    relay(1)
    z_copy.wait_recv()
    sums = part[pl.ds(pl.multiple_of(zh * OWN, OWN), OWN), :] + z_in[...].astype(F32)
    sums = own_x[...].astype(F32) + sums
    resid[...] = sums
    scale = lax.rsqrt(jnp.mean(sums * sums, axis=-1, keepdims=True) + 1e-06)
    ztok[zl] = (sums * scale * moe_gain[...]).astype(BF16)

    def token_copy(r):
        return send_to(
            ztok.at[zl], ztok.at[zl], t_send.at[r], t_recv.at[r], device(x, y, zh * 4 + (zl + r) % 4, c)
        )

    for r in (1, 3, 2):
        token_copy(r).start()
    own_route.wait()
    for r in (1, 2, 3):
        wait_bytes(zroute.at[0], m_recv.at[r])

    def source(pair, b):
        return ((zl // 2 + pair) % 2) * 2 + b

    def spots(b, lane_axis):
        shape = (OWN, SLOTS) if lane_axis else (SLOTS, OWN)
        spot = lax.broadcasted_iota(jnp.int32, shape, 1 if lane_axis else 0) % PAIR
        return (spot - b * CAP).astype(F32)

    def picker(which, lane_axis):
        shape = (128, SLOTS) if lane_axis else (SLOTS, 128)
        expert = lax.broadcasted_iota(jnp.int32, shape, 1 if lane_axis else 0) // PAIR
        field = lax.broadcasted_iota(jnp.int32, shape, 0 if lane_axis else 1)
        return (field == expert + which * 8).astype(F32).astype(BF16)

    def packet(pair, dx, dc):
        to = device(x + dx, y, z, c + dc)
        return send_to(
            packs.at[pair, ((x + dx) % 4) * 2 + (c + dc) % 2], slots.at[pair, x * 2 + c],
            p_send.at[pair], p_recv.at[pair], to,
        )

    def pack(pair):
        hits = []
        for b in range(2):
            place = times(picker(0, False), zroute[source(pair, b)], ((1,), (1,)))
            hits.append(jnp.where(place == spots(b, False), 1.0, 0.0).astype(BF16))
        for n in range(0, WIDTH, WIDE):
            cols = pl.ds(n, WIDE)
            rows = times(hits[0], ztok[source(pair, 0), :, cols]) + times(hits[1], ztok[source(pair, 1), :, cols])
            packs[pair, :, :, cols] = rows.astype(BF16).reshape(8, PAIR, WIDE)
        for dx in (2, 1, 3, 0):
            for dc in (0, 1):
                if dx or dc:
                    packet(pair, dx, dc).start()
        pltpu.make_async_copy(
            packs.at[pair, x * 2 + c], slots.at[pair, x * 2 + c], p_recv.at[pair]
        ).start()

    near_r = (2 * (zl % 2) + 3) % 4
    wait_bytes(ztok.at[0], t_recv.at[near_r])
    pack(0)
    spread(5)
    relay(2)
    for b in range(2):
        wait_bytes(ztok.at[0], t_recv.at[(zl + 4 - source(1, b)) % 4])
    pack(1)
    spread(6)
    relay(3)
    spread(7)

    @pl.loop(4, 8)
    def _(k):
        relay(k)

    for pair in range(2):
        wait_bytes(packs.at[pair, pl.ds(0, 7)], p_send.at[pair])
        wait_bytes(slots.at[pair], p_recv.at[pair])

    def answer(pair, dx, dc):
        to = device(x + dx, y, z, c + dc)
        return send_to(
            packs.at[pair, ((x + dx) % 4) * 2 + (c + dc) % 2], rback.at[pair, x * 2 + c],
            b_send.at[pair], b_recv.at[pair], to,
        )

    def experts(dy, first, last):
        w = ((y + dy) % 4) * 2

        def wide(which, n, count):
            return jnp.concatenate(
                [wbuf[w, which, pl.ds(n, count), :], wbuf[w + 1, which, pl.ds(n, count), :]], axis=1
            )

        @pl.loop(0, 4)
        def _(t):
            pair = 1 - t // 2
            at = pl.ds((t % 2) * 4, 4)
            rows = slots[pair, at].reshape(4 * PAIR, WIDTH)
            gate = times(rows, wide(0, 0, WIDTH))
            up = times(rows, wide(1, 0, WIDTH))
            hidden = (gate * (1.0 / (1.0 + jnp.exp(-gate))) * up).astype(BF16)
            for n in range(0, WIDTH, WIDE):
                cols = pl.ds(n, WIDE)
                got = times(hidden, wide(2, n, WIDE), ((1,), (1,))).reshape(4, PAIR, WIDE)
                if not first:
                    got = got + total[pair, at, :, cols]
                if last:
                    packs[pair, at, :, cols] = got.astype(BF16)
                else:
                    total[pair, at, :, cols] = got

    experts(0, True, False)
    experts(1, False, False)
    experts(3, False, False)
    @pl.loop(0, 8)
    def _(k):
        for way in range(2):
            passed = group(k, 2, way * half, half)
            wait_bytes(passed, r_recv.at[way, k])

    experts(2, False, True)
    for pair in (1, 0):
        for dx in (2, 1, 3, 0):
            for dc in (0, 1):
                if dx or dc:
                    answer(pair, dx, dc).start()
        pltpu.make_async_copy(
            packs.at[pair, x * 2 + c], rback.at[pair, x * 2 + c], b_recv.at[pair]
        ).start()

    def combine(pair):
        wait_bytes(rback.at[pair], b_recv.at[pair])
        for b in range(2):
            from_z = source(pair, b)
            fields = zroute[from_z]
            hit = times(fields, picker(0, True)) == spots(b, True)
            high = jnp.where(hit, times(fields, picker(1, True)), 0.0).astype(BF16)
            low = jnp.where(hit, times(fields, picker(2, True)), 0.0).astype(BF16)
            for n in range(0, WIDTH, WIDE):
                cols = pl.ds(n, WIDE)
                rows = rback[pair, :, :, cols].reshape(SLOTS, WIDE)
                c_out[from_z, :, cols] = (times(high, rows) + times(low, rows)).astype(BF16)

    def back(from_z):
        r = (from_z + 4 - zl) % 4
        return send_to(
            c_out.at[from_z], c_in.at[r], c_send.at[r], c_recv.at[r], device(x, y, zh * 4 + from_z, c)
        )

    combine(1)
    for b in range(2):
        back(source(1, b)).start()
    combine(0)
    near = zl + 1 - 2 * (zl % 2)
    back(near).start()
    result = resid[...] + c_out[zl].astype(F32)
    for r in (1, 3, 2):
        wait_bytes(c_in.at[r], c_recv.at[r])
        result = result + c_in[r].astype(F32)
    out_ref[...] = result.astype(BF16)

    wait_bytes(own_w.at[pl.ds(0, 7)], a_send.at[0])

    @pl.loop(1, 8)
    def _(k):
        wait_bytes(own_w.at[pl.ds(0, 8)], a_send.at[k])

    @pl.loop(0, 8)
    def _(k):
        for way in range(2):
            wait_bytes(group(k, 0), s_send.at[way, k])
            wait_bytes(group(k, 0, 0, half), r_send.at[way, k])

    for r in (1, 2, 3):
        y_copy(r).wait_send()
        token_copy(r).wait_send()
        route_copy(r).wait_send()
        wait_bytes(c_out.at[0], c_send.at[r])
    z_copy.wait_send()
    for pair in range(2):
        wait_bytes(packs.at[pair, pl.ds(0, 7)], b_send.at[pair])


def layer(own_w, x, own_x, attn_gain, w_qkv, w_out, cache, bias, moe_gain, route):
    dma = pltpu.SemaphoreType.DMA
    vmem = pltpu.VMEM
    return pl.pallas_call(
        layer_kernel,
        out_shape=jax.ShapeDtypeStruct((OWN, WIDTH), BF16),
        in_specs=[pl.BlockSpec(memory_space=pltpu.VMEM)] * 10,
        out_specs=pl.BlockSpec(memory_space=pltpu.VMEM),
        scratch_shapes=[
            vmem((8, 3, WIDTH, 128), BF16),
            vmem((ROWS, 6 * HD), BF16),
            vmem((ROWS, 2 * HD), BF16),
            vmem((ROWS // 4, WIDTH), F32),
            vmem((4, ROWS // 4, WIDTH), BF16),
            vmem((4, ROWS // 4, WIDTH), BF16),
            vmem((OWN, WIDTH), BF16),
            vmem((OWN, WIDTH), BF16),
            vmem((OWN, WIDTH), F32),
            vmem((4, OWN, WIDTH), BF16),
            vmem((4, OWN, 128), BF16),
            vmem((2, 8, PAIR, WIDTH), BF16),
            vmem((2, 8, PAIR, WIDTH), BF16),
            vmem((2, 8, PAIR, WIDTH), F32),
            vmem((2, 8, PAIR, WIDTH), BF16),
            vmem((4, OWN, WIDTH), BF16),
            vmem((4, OWN, WIDTH), BF16),
            dma((8,)), dma((8,)),
            dma((2, 8)), dma((2, 8)), dma((2, 8)), dma((2, 8)),
            dma((4,)), dma((4,)), dma, dma,
            dma((4,)), dma((4,)), dma((4,)), dma((4,)),
            dma((2,)), dma((2,)), dma((2,)), dma((2,)), dma((4,)), dma((4,)),
        ],
        compiler_params=pltpu.CompilerParams(
            collective_id=0, has_side_effects=True, vmem_limit_bytes=62 * 1024 * 1024
        ),
        name="layer",
    )(own_w, x, own_x, attn_gain, w_qkv, w_out, cache, bias, moe_gain, route)


def routes(chosen, probs):
    share = probs / jnp.sum(probs, axis=-1, keepdims=True)
    onehot = (chosen[:, :, None] == jnp.arange(EXPERTS, dtype=jnp.int32)).astype(F32)
    named = jnp.sum(onehot, axis=1)
    weight = jnp.sum(onehot * share[:, :, None], axis=1)
    rows = chosen.shape[0]
    earlier = (jnp.arange(rows)[:, None] > jnp.arange(rows)[None, :]).astype(BF16)
    place = jnp.dot(earlier, named.astype(BF16), preferred_element_type=F32)
    place = jnp.where(named > 0, place, -1000.0)
    high = lax.reduce_precision(weight, 8, 7)
    low = weight - high
    fields = jnp.stack([place, high, low], axis=1).reshape(rows, 3, 4, 8)
    fields = fields.transpose(2, 0, 1, 3).reshape(4, rows, 24)
    return jnp.pad(fields, ((0, 0), (0, 0), (0, 104))).astype(BF16)


def on_device(
    x_tokens, attn_gain, w_qkv, w_out, cache, cache_len, moe_gain, w_trainer, expert_ids, route_probs
):
    rows = x_tokens[0]
    own_x = lax.dynamic_slice_in_dim(rows, lax.axis_index("kv") * OWN, OWN, 0)
    live = jnp.arange(CMAX, dtype=jnp.int32)[None, :] < cache_len[:, None]
    bias = jnp.where(live, 0.0, -1e30).astype(F32)
    out = layer(
        w_trainer.astype(BF16), rows, own_x, attn_gain[None], w_qkv.reshape(WIDTH, -1), w_out, cache, bias,
        moe_gain[None], routes(expert_ids[0], route_probs[0]),
    )
    return out[None]


def solution(mesh):
    return jax.shard_map(
        on_device,
        mesh=mesh,
        in_specs=(
            P("ex", None, None),
            P(),
            P(None, None, "kv"),
            P("kv", None),
            P("ex", None, None, "kv"),
            P("ex"),
            P(),
            P(None, None, "ex", "kv"),
            P("ex", "kv", None),
            P("ex", "kv", None),
        ),
        out_specs=P("ex", "kv", None),
        check_vma=False,
    )
```

```python
import math

import jax
import jax.numpy as jnp
from jax import lax
from jax.experimental import pallas as pl
from jax.experimental.pallas import tpu as pltpu
from jax.sharding import PartitionSpec as P

HD = 128
TOPK = 8
PLEN = 512
REQ_DEV = 2
QB = 32
CMAX = 512
EXPERTS = 32
CAP = 28
WIDTH = 2048
ROWS = 576
OWN = 72
PAIR = 2 * CAP
SLOTS = 8 * PAIR
WIDE = 512
MESH = pl.DeviceIdType.MESH
F32 = jnp.float32
BF16 = jnp.bfloat16


def position():
    kv, ex = lax.axis_index("kv"), lax.axis_index("ex")
    return (ex // 2) % 4, kv // 2, (kv % 2) * 4 + ex // 8, ex % 2


def device(x, y, z, c):
    x, y, z, c = (x + 8) % 4, (y + 8) % 4, (z + 16) % 8, c % 2
    return y * 2 + z // 4, ((z % 4) * 4 + x) * 2 + c


def send_to(src, dst, send_sem, recv_sem, to):
    return pltpu.make_async_remote_copy(
        src_ref=src, dst_ref=dst, send_sem=send_sem, recv_sem=recv_sem, device_id=to, device_id_type=MESH
    )


def wait_bytes(ref, sem):
    pltpu.make_async_copy(ref, ref, sem).wait()


def times(a, b, contract=((1,), (0,))):
    return lax.dot_general(a, b, (contract, ((), ())), preferred_element_type=F32)


def softmax(parts):
    top = parts[0].max(axis=-1, keepdims=True)
    for part in parts[1:]:
        top = jnp.maximum(top, part.max(axis=-1, keepdims=True))
    parts = [jnp.exp(part - top) for part in parts]
    total = parts[0].sum(axis=-1, keepdims=True)
    for part in parts[1:]:
        total = total + part.sum(axis=-1, keepdims=True)
    return [(part / total).astype(BF16) for part in parts]


def layer_kernel(
    trainer_hbm, x_hbm, attn_gain, qkv_hbm, wout_hbm, cache_hbm, bias, moe_gain, route,
    out_ref,
    raw, own_w, x_ref, own_x, w_qkv, w_out, cache, wbuf, proj, heads, part, y_out, y_in, z_out, z_in, resid, ztok, zroute, packs, slots, total, rback, c_out, c_in,
    a_send, a_recv, s_send, s_recv, r_send, r_recv, y_send, y_recv, z_send, z_recv,
    t_send, t_recv, u_send, u_recv, m_send, m_recv, p_send, p_recv, b_send, b_recv, c_send, c_recv,
    raw_sem, in_sem,
):
    x, y, z, c = position()
    kv, ex = device(x, y, z, c)
    zl, zh = z % 4, z // 4
    piece_rows = own_w.shape[2]
    barrier = pltpu.get_barrier_semaphore()

    def raw_copy(i):
        return pltpu.make_async_copy(trainer_hbm.at[pl.ds(i * 8, 8)], raw.at[i % 2], raw_sem.at[i % 2])

    loads = [
        pltpu.make_async_copy(x_hbm, x_ref, in_sem.at[0]),
        pltpu.make_async_copy(qkv_hbm, w_qkv, in_sem.at[1]),
        pltpu.make_async_copy(cache_hbm, cache, in_sem.at[2]),
        pltpu.make_async_copy(wout_hbm, w_out, in_sem.at[3]),
        pltpu.make_async_copy(x_hbm.at[pl.ds(pl.multiple_of(kv * OWN, 8), OWN)], own_x, in_sem.at[4]),
    ]
    raw_copy(0).start()
    raw_copy(1).start()
    for load in loads:
        load.start()

    @pl.loop(0, 8)
    def _(k):
        for dx in range(4):
            for dc in range(2):
                if dx or dc:
                    pl.semaphore_signal(
                        barrier, inc=1, device_id=device(x + dx, y, z + k, c + dc), device_id_type=MESH
                    )

    @pl.loop(1, 8)
    def _(k):
        pl.semaphore_signal(barrier, inc=1, device_id=device(x, y, z + k, c), device_id_type=MESH)

    for dy in (1, 2, 3):
        pl.semaphore_signal(barrier, inc=1, device_id=device(x, y + dy, z, c), device_id_type=MESH)
    for i in range(4):
        raw_copy(i).wait()
        own_w[pl.ds(i * 8, 8)] = raw[i % 2].astype(BF16)
        if i < 2:
            raw_copy(i + 2).start()
    pl.semaphore_wait(barrier, 66)

    def route_copy(r):
        return send_to(
            route.at[(zl + r) % 4], zroute.at[zl], m_send.at[r], m_recv.at[r],
            device(x, y, zh * 4 + (zl + r) % 4, c),
        )

    for r in (1, 2, 3):
        route_copy(r).start()
    own_route = pltpu.make_async_copy(route.at[zl], zroute.at[zl], m_recv.at[0])
    own_route.start()

    own_rows = pl.ds(pl.multiple_of(ex * piece_rows, piece_rows), piece_rows)

    def piece(k, dx, dc):
        to = device(x + dx, y, z + (3 * k) % 8, c + dc)
        return send_to(own_w.at[to[1]], wbuf.at[kv, :, own_rows, :], a_send.at[k], a_recv.at[k], to)

    pltpu.make_async_copy(own_w.at[ex], wbuf.at[kv, :, own_rows, :], a_recv.at[0]).start()
    for dx in (1, 3, 2, 0):
        for dc in (0, 1):
            if dx or dc:
                piece(0, dx, dc).start()

    @pl.loop(1, 8)
    def _(k):
        for dx in (1, 3, 2, 0):
            for dc in (0, 1):
                piece(k, dx, dc).start()

    whole = 8 * piece_rows

    def group(k, dy, first=0, count=whole):
        zs = (z + 8 - (3 * k) % 8) % 8
        begin = pl.multiple_of((zs % 4) * whole + first, piece_rows)
        return wbuf.at[((y + dy) % 4) * 2 + zs // 4, :, pl.ds(begin, count), :]

    half = whole // 2

    def spread(k):
        wait_bytes(group(k, 0), a_recv.at[k])
        for way, dy in ((0, 1), (1, 3)):
            send_to(
                group(k, 0), group(k, 0), s_send.at[way, k], s_recv.at[way, k], device(x, y + dy, z, c)
            ).start()

    def relay(k):
        for way, dy in ((0, 1), (1, 3)):
            wait_bytes(group(k, 4 - dy), s_recv.at[way, k])
            passed = group(k, 4 - dy, way * half, half)
            send_to(passed, passed, r_send.at[way, k], r_recv.at[way, k], device(x, y + dy, z, c)).start()

    loads[0].wait()
    loads[1].wait()

    @pl.loop(0, 2)
    def _(i):
        rows = pl.ds(pl.multiple_of(i * (ROWS // 2), ROWS // 2), ROWS // 2)
        values = x_ref[rows, :].astype(F32)
        scale = lax.rsqrt(jnp.mean(values * values, axis=-1, keepdims=True) + 1e-06)
        normed = (values * scale * attn_gain[...]).astype(BF16)
        for which in range(3):
            proj[rows, pl.ds(which * 2 * HD, 2 * HD)] = times(normed, w_qkv[which]).astype(BF16)

    for load in loads[2:]:
        load.wait()

    spread(0)

    def lanes(which, head):
        return pl.ds((which * 2 + head) * HD, HD)

    inv = 1.0 / math.sqrt(HD)
    tile = 128
    for head in range(2):
        @pl.loop(0, PLEN // tile)
        def _(i):
            rows = pl.ds(pl.multiple_of(i * tile, tile), tile)
            scores = times(proj[rows, lanes(0, head)], proj[0:PLEN, lanes(1, head)], ((1,), (1,))) * inv
            (probs,) = softmax([scores])
            heads[rows, pl.ds(head * HD, HD)] = times(probs, proj[0:PLEN, lanes(2, head)]).astype(BF16)

        for req in range(REQ_DEV):
            rows = pl.ds(PLEN + req * QB, QB)
            query = proj[rows, lanes(0, head)]
            near = times(query, proj[rows, lanes(1, head)], ((1,), (1,))) * inv
            far = times(query, cache[req, 0, :, pl.ds(head * HD, HD)], ((1,), (1,))) * inv
            far = far + bias[req:req + 1, :]
            near, far = softmax([near, far])
            mixed = times(near, proj[rows, lanes(2, head)]) + times(far, cache[req, 1, :, pl.ds(head * HD, HD)])
            heads[rows, pl.ds(head * HD, HD)] = mixed.astype(BF16)
        spread(1 + head)

    quarter = ROWS // 4

    def block(dy):
        return heads[pl.ds(pl.multiple_of(((y + dy) % 4) * quarter, quarter), quarter), :]

    def y_copy(dy):
        return send_to(y_out.at[dy], y_in.at[dy], y_send.at[dy], y_recv.at[dy], device(x, y + dy, z, c))

    for dy in (2, 1, 3):
        y_out[dy] = times(block(dy), w_out[...]).astype(BF16)
        y_copy(dy).start()
    part[...] = times(block(0), w_out[...])
    spread(3)
    relay(0)
    for dy in (1, 3, 2):
        y_copy(dy).wait_recv()
        part[...] += y_in[dy].astype(F32)
    z_out[...] = part[pl.ds(pl.multiple_of((1 - zh) * OWN, OWN), OWN), :].astype(BF16)
    z_copy = send_to(z_out, z_in, z_send, z_recv, device(x, y, z + 4, c))
    z_copy.start()
    spread(4)
    relay(1)
    z_copy.wait_recv()
    sums = part[pl.ds(pl.multiple_of(zh * OWN, OWN), OWN), :] + z_in[...].astype(F32)
    sums = own_x[...].astype(F32) + sums
    resid[...] = sums
    scale = lax.rsqrt(jnp.mean(sums * sums, axis=-1, keepdims=True) + 1e-06)
    ztok[zl] = (sums * scale * moe_gain[...]).astype(BF16)

    near = zl + 1 - 2 * (zl % 2)
    inner = (zl + 1) % 4 // 2
    far_inner = (2 - zl // 2)

    def column(to):
        return device(x, y, zh * 4 + to, c)

    def near_copy():
        return send_to(ztok.at[zl], ztok.at[zl], t_send.at[0], t_recv.at[0], column(near))

    def far_copy():
        return send_to(ztok.at[zl], ztok.at[zl], t_send.at[1], t_recv.at[1 + inner], column(far_inner))

    def pass_on(b):
        block = source(1, b)
        return send_to(ztok.at[block], ztok.at[block], u_send.at[b], u_recv.at[b], column(near))

    near_copy().start()
    far_copy().start()
    own_route.wait()
    for r in (1, 2, 3):
        wait_bytes(zroute.at[0], m_recv.at[r])

    def source(pair, b):
        return ((zl // 2 + pair) % 2) * 2 + b

    def spots(b, lane_axis):
        shape = (OWN, SLOTS) if lane_axis else (SLOTS, OWN)
        spot = lax.broadcasted_iota(jnp.int32, shape, 1 if lane_axis else 0) % PAIR
        return (spot - b * CAP).astype(F32)

    def picker(which, lane_axis):
        shape = (128, SLOTS) if lane_axis else (SLOTS, 128)
        expert = lax.broadcasted_iota(jnp.int32, shape, 1 if lane_axis else 0) // PAIR
        field = lax.broadcasted_iota(jnp.int32, shape, 0 if lane_axis else 1)
        return (field == expert + which * 8).astype(F32).astype(BF16)

    def packet(pair, dx, dc):
        to = device(x + dx, y, z, c + dc)
        return send_to(
            packs.at[pair, ((x + dx) % 4) * 2 + (c + dc) % 2], slots.at[pair, x * 2 + c],
            p_send.at[pair], p_recv.at[pair], to,
        )

    def pack(pair):
        hits = []
        for b in range(2):
            place = times(picker(0, False), zroute[source(pair, b)], ((1,), (1,)))
            hits.append(jnp.where(place == spots(b, False), 1.0, 0.0).astype(BF16))
        for n in range(0, WIDTH, WIDE):
            cols = pl.ds(n, WIDE)
            rows = times(hits[0], ztok[source(pair, 0), :, cols]) + times(hits[1], ztok[source(pair, 1), :, cols])
            packs[pair, :, :, cols] = rows.astype(BF16).reshape(8, PAIR, WIDE)
        for dx in (2, 1, 3, 0):
            for dc in (0, 1):
                if dx or dc:
                    packet(pair, dx, dc).start()
        pltpu.make_async_copy(
            packs.at[pair, x * 2 + c], slots.at[pair, x * 2 + c], p_recv.at[pair]
        ).start()

    wait_bytes(ztok.at[0], t_recv.at[0])
    pack(0)

    @pl.when(inner == 1)
    def _():
        wait_bytes(ztok.at[0], t_recv.at[2])
        pass_on(zl // 2).start()
        wait_bytes(ztok.at[0], t_recv.at[1])
        pass_on(1 - zl // 2).start()

    spread(5)
    relay(2)

    @pl.when(inner == 0)
    def _():
        for b in range(2):
            wait_bytes(ztok.at[0], u_recv.at[b])

    pack(1)
    spread(6)
    relay(3)
    spread(7)

    @pl.loop(4, 8)
    def _(k):
        relay(k)

    for pair in range(2):
        wait_bytes(packs.at[pair, pl.ds(0, 7)], p_send.at[pair])
        wait_bytes(slots.at[pair], p_recv.at[pair])

    def answer(pair, dx, dc):
        to = device(x + dx, y, z, c + dc)
        return send_to(
            packs.at[pair, ((x + dx) % 4) * 2 + (c + dc) % 2], rback.at[pair, x * 2 + c],
            b_send.at[pair], b_recv.at[pair], to,
        )

    def experts(dy, first, last):
        w = ((y + dy) % 4) * 2

        def wide(which, n, count):
            return jnp.concatenate(
                [wbuf[w, which, pl.ds(n, count), :], wbuf[w + 1, which, pl.ds(n, count), :]], axis=1
            )

        def step(pair, t):
            at = pl.ds(t * 4, 4)
            rows = slots[pair, at].reshape(4 * PAIR, WIDTH)
            gate = times(rows, wide(0, 0, WIDTH))
            up = times(rows, wide(1, 0, WIDTH))
            hidden = (gate * (1.0 / (1.0 + jnp.exp(-gate))) * up).astype(BF16)
            for n in range(0, WIDTH, WIDE):
                cols = pl.ds(n, WIDE)
                got = times(hidden, wide(2, n, WIDE), ((1,), (1,))).reshape(4, PAIR, WIDE)
                if not first:
                    got = got + total[pair, at, :, cols]
                if last:
                    packs[pair, at, :, cols] = got.astype(BF16)
                else:
                    total[pair, at, :, cols] = got

        if last:
            for pair in (1, 0):
                pl.loop(0, 2)(lambda t: step(pair, t))
                for dx in (2, 1, 3, 0):
                    for dc in (0, 1):
                        if dx or dc:
                            answer(pair, dx, dc).start()
                pltpu.make_async_copy(
                    packs.at[pair, x * 2 + c], rback.at[pair, x * 2 + c], b_recv.at[pair]
                ).start()
        else:
            pl.loop(0, 4)(lambda t: step(t // 2, t % 2))

    experts(0, True, False)
    experts(1, False, False)
    experts(3, False, False)

    @pl.loop(0, 8)
    def _(k):
        for way in range(2):
            passed = group(k, 2, way * half, half)
            wait_bytes(passed, r_recv.at[way, k])

    experts(2, False, True)

    def combine(pair):
        wait_bytes(rback.at[pair], b_recv.at[pair])
        for b in range(2):
            from_z = source(pair, b)
            fields = zroute[from_z]
            hit = times(fields, picker(0, True)) == spots(b, True)
            high = jnp.where(hit, times(fields, picker(1, True)), 0.0).astype(BF16)
            low = jnp.where(hit, times(fields, picker(2, True)), 0.0).astype(BF16)
            for n in range(0, WIDTH, WIDE):
                cols = pl.ds(n, WIDE)
                rows = rback[pair, :, :, cols].reshape(SLOTS, WIDE)
                c_out[from_z, :, cols] = (times(high, rows) + times(low, rows)).astype(BF16)

    def back(from_z):
        r = (from_z + 4 - zl) % 4
        return send_to(
            c_out.at[from_z], c_in.at[r], c_send.at[r], c_recv.at[r], device(x, y, zh * 4 + from_z, c)
        )

    combine(1)
    for b in range(2):
        back(source(1, b)).start()
    combine(0)
    back(near).start()
    result = resid[...] + c_out[zl].astype(F32)
    for r in (1, 3, 2):
        wait_bytes(c_in.at[r], c_recv.at[r])
        result = result + c_in[r].astype(F32)
    out_ref[...] = result.astype(BF16)

    wait_bytes(own_w.at[pl.ds(0, 7)], a_send.at[0])

    @pl.loop(1, 8)
    def _(k):
        wait_bytes(own_w.at[pl.ds(0, 8)], a_send.at[k])

    @pl.loop(0, 8)
    def _(k):
        for way in range(2):
            wait_bytes(group(k, 0), s_send.at[way, k])
            wait_bytes(group(k, 0, 0, half), r_send.at[way, k])

    for r in (1, 2, 3):
        y_copy(r).wait_send()
        route_copy(r).wait_send()
        wait_bytes(c_out.at[0], c_send.at[r])
    z_copy.wait_send()
    near_copy().wait_send()
    far_copy().wait_send()

    @pl.when(inner == 1)
    def _():
        for b in range(2):
            pass_on(b).wait_send()

    for pair in range(2):
        wait_bytes(packs.at[pair, pl.ds(0, 7)], b_send.at[pair])


def layer(trainer, x, attn_gain, w_qkv, w_out, cache, bias, moe_gain, route):
    dma = pltpu.SemaphoreType.DMA
    vmem = pltpu.VMEM
    anywhere, held = pl.BlockSpec(memory_space=pl.ANY), pl.BlockSpec(memory_space=pltpu.VMEM)
    return pl.pallas_call(
        layer_kernel,
        out_shape=jax.ShapeDtypeStruct((OWN, WIDTH), BF16),
        in_specs=[anywhere, anywhere, held, anywhere, anywhere, anywhere, held, held, held],
        out_specs=held,
        scratch_shapes=[
            vmem((2, 8) + trainer.shape[1:], F32),
            vmem(trainer.shape, BF16),
            vmem(x.shape, BF16),
            vmem((OWN, WIDTH), BF16),
            vmem(w_qkv.shape, BF16),
            vmem(w_out.shape, BF16),
            vmem(cache.shape, BF16),
            vmem((8, 3, WIDTH, 128), BF16),
            vmem((ROWS, 6 * HD), BF16),
            vmem((ROWS, 2 * HD), BF16),
            vmem((ROWS // 4, WIDTH), F32),
            vmem((4, ROWS // 4, WIDTH), BF16),
            vmem((4, ROWS // 4, WIDTH), BF16),
            vmem((OWN, WIDTH), BF16),
            vmem((OWN, WIDTH), BF16),
            vmem((OWN, WIDTH), F32),
            vmem((4, OWN, WIDTH), BF16),
            vmem((4, OWN, 128), BF16),
            vmem((2, 8, PAIR, WIDTH), BF16),
            vmem((2, 8, PAIR, WIDTH), BF16),
            vmem((2, 8, PAIR, WIDTH), F32),
            vmem((2, 8, PAIR, WIDTH), BF16),
            vmem((4, OWN, WIDTH), BF16),
            vmem((4, OWN, WIDTH), BF16),
            dma((8,)), dma((8,)),
            dma((2, 8)), dma((2, 8)), dma((2, 8)), dma((2, 8)),
            dma((4,)), dma((4,)), dma, dma,
            dma((2,)), dma((3,)), dma((2,)), dma((2,)), dma((4,)), dma((4,)),
            dma((2,)), dma((2,)), dma((2,)), dma((2,)), dma((4,)), dma((4,)),
            dma((2,)), dma((5,)),
        ],
        compiler_params=pltpu.CompilerParams(
            collective_id=0, has_side_effects=True, vmem_limit_bytes=62 * 1024 * 1024
        ),
        name="layer",
    )(trainer, x, attn_gain, w_qkv, w_out, cache, bias, moe_gain, route)


def routes(chosen, probs):
    share = probs / jnp.sum(probs, axis=-1, keepdims=True)
    onehot = (chosen[:, :, None] == jnp.arange(EXPERTS, dtype=jnp.int32)).astype(F32)
    named = jnp.sum(onehot, axis=1)
    weight = jnp.sum(onehot * share[:, :, None], axis=1)
    rows = chosen.shape[0]
    earlier = (jnp.arange(rows)[:, None] > jnp.arange(rows)[None, :]).astype(BF16)
    place = jnp.dot(earlier, named.astype(BF16), preferred_element_type=F32)
    place = jnp.where(named > 0, place, -1000.0)
    high = lax.reduce_precision(weight, 8, 7)
    low = weight - high
    fields = jnp.stack([place, high, low], axis=1).reshape(rows, 3, 4, 8)
    fields = fields.transpose(2, 0, 1, 3).reshape(4, rows, 24)
    return jnp.pad(fields, ((0, 0), (0, 0), (0, 104))).astype(BF16)


def on_device(
    x_tokens, attn_gain, w_qkv, w_out, cache, cache_len, moe_gain, w_trainer, expert_ids, route_probs
):
    rows = x_tokens[0]
    live = jnp.arange(CMAX, dtype=jnp.int32)[None, :] < cache_len[:, None]
    bias = jnp.where(live, 0.0, -1e30).astype(F32)
    out = layer(
        w_trainer, rows, attn_gain[None], w_qkv.transpose(1, 0, 2), w_out, cache, bias,
        moe_gain[None], routes(expert_ids[0], route_probs[0]),
    )
    return out[None]


def solution(mesh):
    return jax.shard_map(
        on_device,
        mesh=mesh,
        in_specs=(
            P("ex", None, None),
            P(),
            P(None, None, "kv"),
            P("kv", None),
            P("ex", None, None, "kv"),
            P("ex"),
            P(),
            P(None, None, "ex", "kv"),
            P("ex", "kv", None),
            P("ex", "kv", None),
        ),
        out_specs=P("ex", "kv", None),
        check_vma=False,
    )
```
